256 devices in a mesh: gx: 8 (over x, core), gy: 32 (over y, z).
Axes of the slice: x: 4, y: 4, z: 8, core: 2. Of those that a mesh axis runs over, the one named last changes fastest.
Arguments:
- fields: bfloat16 [672, 672, 1536], P('gx', 'gy'), may hold values from -16 to 16
- x_factor: bfloat16 [672, 336], replicated, may hold values from -0.00030517578 to 0.00030517578
- running_r: float32 [672, 672], replicated, as said below
Outputs:
- new_r: float32 [672, 672], P('gy', 'gx')
The draws below stay inside these ranges and needn't reach their ends.
Inputs may be any that keep to these rules, and one draw needn't show every extreme that they name: `running_r`: upper triangular with a positive diagonal.
All inputs are finite; a program needn't handle non-finite values.
Results may differ from the reference program's by a relative error of at most 0.0003.
Values may be sent and summed in bfloat16 or wider, within the bound.
A program may use at most 256 MiB of HBM per device.

```python
import jax
import jax.numpy as jnp
from jax import lax

NX = 672
NY = 672
NR = 336
CELLS = 1536


def draw_running_r(key, part):
    first, second = jax.random.split(jax.random.fold_in(key, 7))
    upper = jax.random.normal(first, (NY, NY), jnp.float32) * NY ** (-0.5)
    diag_vals = jnp.exp(jax.random.uniform(second, (NY,), jnp.float32, jnp.log(0.5), jnp.log(2.0)))
    return jnp.triu(upper, 1) + jnp.diag(diag_vals)


def draw_fields(key, part):
    first = jax.random.fold_in(jax.random.fold_in(key, 11), 0)
    values = jnp.clip(jax.random.normal(first, (NX, NY, CELLS), jnp.float32), -6.0, 6.0)
    return values.astype(jnp.bfloat16)


def bell_draw(stream_key, dims, spread, reach, held_as=jnp.bfloat16):
    values = jax.random.normal(stream_key, dims, jnp.float32) * spread
    return jnp.minimum(jnp.maximum(values, -reach), reach).astype(held_as)


def setup_inputs(seed: int = 0) -> dict:
    arg_keys = jax.random.split(jax.random.key(seed), 4)
    fields = draw_fields(jax.random.fold_in(arg_keys[3], 71), 0)
    x_factor = bell_draw(arg_keys[1], (NX, NR), (NX * NR * CELLS) ** -0.5, 0.00030517578)
    running_r = draw_running_r(jax.random.fold_in(arg_keys[3], 71), 0)
    return {"fields": fields, "x_factor": x_factor, "running_r": running_r}


def reference(fields, x_factor, running_r):

    def one_block(gram_sum, index):
        block = lax.dynamic_slice_in_dim(fields, (index * 128).astype(jnp.int32), 128, 2)
        projected = lax.dot_general(x_factor.astype(jnp.float32), block.reshape(NX, NY * 128).astype(jnp.float32), (((0,), (0,)), ((), ())), preferred_element_type=jnp.float32).astype(jnp.bfloat16)
        wide = projected.reshape(NR, NY, 128).astype(jnp.float32)
        return (gram_sum + jnp.einsum('ayc,azc->yz', wide, wide, precision=lax.Precision.HIGHEST), None)
    start_gram = jnp.zeros((NY, NY), jnp.float32)
    gram_sum, _ = lax.scan(one_block, start_gram, jnp.arange(CELLS // 128, dtype=jnp.int32))
    total = jnp.dot(running_r.T.astype(jnp.float32), running_r.astype(jnp.float32), precision=lax.Precision.HIGHEST, preferred_element_type=jnp.float32) + gram_sum
    return jnp.linalg.cholesky(total).T
```

```python
import functools

import jax
import jax.numpy as jnp
from jax import lax
from jax.experimental import pallas as pl
from jax.experimental.pallas import tpu as pltpu
from jax.sharding import PartitionSpec as P

MESH = pl.DeviceIdType.MESH
LANES = 128
ROWS = 8
UNIT = 16
HIGH = lax.Precision.HIGHEST


def round_up(value, step):
    return -(-value // step) * step


class Plan:
    def __init__(self, n_gx, n_gy, x_block, y_block, cells, rank, full_y):
        self.n_gx, self.n_gy = n_gx, n_gy
        self.chips = n_gx // 2
        self.x_block = x_block
        self.x_pad = round_up(x_block, 32)
        self.y_block = y_block
        self.y_first = (y_block + 1) // 2
        self.y_common = y_block // 2
        self.cell_tiles = cells // LANES // self.chips
        self.part_cells = self.cell_tiles * LANES
        self.rank = rank
        self.rank_units = rank // UNIT
        self.units = self.cell_tiles * self.rank_units
        self.full_y = full_y
        self.y_lanes = round_up(full_y, LANES)
        self.chunks = self.make_chunks()
        tiles = []
        for row in range(0, full_y, ROWS):
            for tile in range(row // LANES, self.y_lanes // LANES):
                tiles.append((row, tile))
        self.tiles = tiles
        owners = min(n_gy, -(-len(tiles) // (2 * n_gx)))
        self.per_owner = -(-len(tiles) // (n_gx * owners))
        self.owners = -(-len(tiles) // (n_gx * self.per_owner))
        self.piece = self.per_owner * self.owners
        self.half = self.piece * self.chips
        self.n_tiles = 2 * self.half

    def make_chunks(self):
        count = min(5, self.y_common)
        bounds = [self.y_common * i // count for i in range(count + 1)]
        return [(low, high - low) for low, high in zip(bounds[:-1], bounds[1:])]


def exchange_kernel(
    plan, f_hbm, xt_ref, r_ref, out_ref,
    fbuf, fibres, pbuf, gbuf, mbuf, gram, tiles, summed, core_in, x_in, y_in,
    s1_send, s1_recv, s2_send, s2_recv, e_send, e_recv, rs_send, rs_recv, loc,
):
    n_gx, n_gy, chips = plan.n_gx, plan.n_gy, plan.chips
    gx = lax.axis_index("gx")
    gy = lax.axis_index("gy")
    xi = gx // 2
    core = gx % 2
    units = plan.units
    has_extra = plan.y_first > plan.y_common
    extra_slot = len(plan.chunks)

    def remote(src, dst, send, recv, to_gx, to_gy):
        return pltpu.make_async_remote_copy(
            src_ref=src, dst_ref=dst, send_sem=send, recv_sem=recv,
            device_id=(to_gx, to_gy), device_id_type=MESH,
        )

    barrier = pltpu.get_barrier_semaphore()

    @pl.loop(1, n_gx)
    def _(step):
        pl.semaphore_signal(barrier, inc=1, device_id=(lax.rem(gx + step, n_gx), gy), device_id_type=MESH)

    @pl.loop(1, n_gy)
    def _(step):
        to_gy = lax.rem(gy + step, n_gy)
        pl.semaphore_signal(barrier, inc=1, device_id=(2 * xi, to_gy), device_id_type=MESH)
        pl.semaphore_signal(barrier, inc=1, device_id=(2 * xi + 1, to_gy), device_id_type=MESH)

    if plan.x_pad > plan.x_block:
        for block in range(n_gx):
            low = block * plan.x_pad + plan.x_block
            high = (block + 1) * plan.x_pad
            fibres[low:high, :] = jnp.zeros((high - low, plan.part_cells), jnp.bfloat16)

    pl.semaphore_wait(barrier, (n_gx - 1) + 2 * (n_gy - 1))

    def field_src(to_core, to_chip, low, size):
        return f_hbm.at[
            pl.ds(plan.y_first * to_core + low, size), :,
            pl.ds(pl.multiple_of(plan.part_cells * to_chip, LANES), plan.part_cells),
        ]

    def field_dst(low, size):
        return fbuf.at[pl.ds(low, size), gx]

    def stage1(index, low, size):
        local = pltpu.make_async_copy(
            field_src(core, xi, low, size), field_dst(low, size), s1_recv.at[index, gx]
        )
        local.start()

        @pl.loop(1, n_gx)
        def _(step):
            to = lax.rem(gx + step, n_gx)
            remote(
                field_src(to % 2, to // 2, low, size), field_dst(low, size),
                s1_send.at[index], s1_recv.at[index, gx], to, gy,
            ).start()

    for index, (low, size) in enumerate(plan.chunks):
        stage1(index, low, size)
    low_extra = plan.y_common
    if has_extra:
        @pl.loop(1, chips)
        def _(step):
            to_chip = lax.rem(xi + step, chips)
            remote(
                field_src(0, to_chip, low_extra, 1), field_dst(low_extra, 1),
                s1_send.at[extra_slot], s1_recv.at[extra_slot, gx], 2 * to_chip, gy,
            ).start()

        @pl.when(core == 0)
        def _():
            pltpu.make_async_copy(
                field_src(0, xi, low_extra, 1), field_dst(low_extra, 1), s1_recv.at[extra_slot, gx]
            ).start()

        @pl.when(core == 1)
        def _():
            remote(
                field_src(0, xi, low_extra, 1), field_dst(low_extra, 1),
                s1_send.at[extra_slot], s1_recv.at[extra_slot, gx], 2 * xi, gy,
            ).start()

    def project(y):
        for block in range(n_gx):
            low = block * plan.x_pad
            fibres[low:low + plan.x_block, :] = fbuf[y, block]
        product = jnp.dot(xt_ref[...], fibres[...], preferred_element_type=jnp.float32).astype(jnp.bfloat16)
        for tile in range(plan.cell_tiles):
            part = product[:, tile * LANES:(tile + 1) * LANES]
            pbuf[y, pl.ds(tile * plan.rank_units, plan.rank_units)] = part.reshape(plan.rank_units, UNIT, LANES)

    def tile_src(unit, low, size):
        return pbuf.at[pl.ds(low, size), lax.rem(unit, units)]

    def tile_dst(low, size):
        return gbuf.at[pl.ds(plan.y_block * gy + plan.y_first * core + low, size)]

    def stage2(low, size, send, recv):
        pltpu.make_async_copy(tile_src(2 * gy + core, low, size), tile_dst(low, size), recv).start()
        remote(
            tile_src(2 * gy + 1 - core, low, size), tile_dst(low, size), send, recv, 2 * xi + 1 - core, gy
        ).start()

        @pl.loop(1, n_gy)
        def _(step):
            to_gy = lax.rem(gy + step, n_gy)
            for to_core in range(2):
                remote(
                    tile_src(2 * to_gy + to_core, low, size), tile_dst(low, size), send, recv,
                    2 * xi + to_core, to_gy,
                ).start()

    def chunk_done(index, low, size):
        for source in range(n_gx):
            there = fbuf.at[pl.ds(low, size), source]
            pltpu.make_async_copy(there, there, s1_recv.at[index, source]).wait()

    for index, (low, size) in enumerate(plan.chunks):
        chunk_done(index, low, size)

        @pl.loop(low, low + size)
        def _(y):
            project(y)

        stage2(low, size, s2_send, s2_recv)

    if has_extra:
        @pl.when(core == 0)
        def _():
            chunk_done(extra_slot, low_extra, 1)
            project(low_extra)
            stage2(low_extra, 1, e_send, s2_recv)

    n_y = plan.full_y
    for low in range(0, n_y, LANES):
        high = min(low + LANES, n_y)
        out_ref[low:high, low:n_y] = lax.dot_general(
            r_ref[0:high, low:high], r_ref[0:high, low:n_y], (((0,), (0,)), ((), ())),
            precision=HIGH, preferred_element_type=jnp.float32,
        )
        if low:
            out_ref[low:high, 0:low] = jnp.zeros((high - low, low), jnp.float32)

    size = UNIT * UNIT
    to_row = lax.broadcasted_iota(jnp.int32, (size, size), 0)
    from_row = lax.broadcasted_iota(jnp.int32, (size, size), 1)
    turn = ((to_row % UNIT == from_row // UNIT) & (to_row // UNIT == from_row % UNIT)).astype(jnp.bfloat16)

    pltpu.make_async_copy(gbuf, gbuf, s2_recv).wait()

    @pl.loop(0, n_y // UNIT)
    def _(group):
        rows = pl.ds(pl.multiple_of(group * UNIT, UNIT), UNIT)
        block = gbuf[rows].reshape(size, LANES)
        turned = jnp.dot(turn, block, preferred_element_type=jnp.float32).astype(jnp.bfloat16)
        turned = turned.reshape(UNIT, UNIT, LANES)
        for a in range(UNIT):
            mbuf[a // 2, rows, (a % 2) * LANES:(a % 2 + 1) * LANES] = turned[a]

    keep = jnp.where(2 * gy + core < units, 1.0, 0.0).astype(jnp.float32)
    for low in range(0, n_y, LANES):
        high = min(low + LANES, n_y)
        total = jnp.zeros((high - low, n_y - low), jnp.float32)
        for a in range(UNIT // 2):
            total = total + lax.dot_general(
                mbuf[a, low:high, :], mbuf[a, low:n_y, :], (((1,), (1,)), ((), ())),
                preferred_element_type=jnp.float32,
            )
        gram[low:high, low:n_y] = total * keep

    gap = plan.y_lanes - n_y
    for index, (row, tile) in enumerate(plan.tiles):
        width = min(LANES, n_y - tile * LANES)
        if width < LANES:
            tiles[index] = jnp.zeros((ROWS, LANES), jnp.float32)
        tiles[index, :, 0:width] = gram[row:row + ROWS, tile * LANES:tile * LANES + width]
    for index in range(len(plan.tiles), plan.n_tiles):
        tiles[index] = jnp.zeros((ROWS, LANES), jnp.float32)

    half, piece, own = plan.half, plan.piece, plan.per_owner
    my_half = core * half
    other_half = (1 - core) * half
    send = remote(
        tiles.at[pl.ds(other_half, half)], core_in, rs_send.at[0], rs_recv.at[0], 2 * xi + 1 - core, gy
    )
    send.start()
    send.wait()

    def add_core(i):
        tiles[my_half + i] += core_in[i]
    pl.loop(0, half)(add_core)

    x_sends = []
    for step in range(1, chips):
        to = lax.rem(xi + step, chips)
        send = remote(
            tiles.at[pl.ds(my_half + to * piece, piece)], x_in.at[step], rs_send.at[1], rs_recv.at[step],
            2 * to + core, gy,
        )
        send.start()
        x_sends.append(send)
    for send in x_sends:
        send.wait_recv()
    my_piece = my_half + xi * piece

    def add_x(i):
        value = tiles[my_piece + i]
        for step in range(1, chips):
            value = value + x_in[step, i]
        tiles[my_piece + i] = value
    pl.loop(0, piece)(add_x)

    @pl.loop(1, n_gy)
    def _(step):
        to = lax.rem(gy + step, n_gy)

        @pl.when(to < plan.owners)
        def _():
            remote(
                tiles.at[pl.ds(my_piece + to * own, own)], y_in.at[pl.ds(gy * own, own)], rs_send.at[2], rs_recv.at[chips],
                gx, to,
            ).start()

    @pl.when(gy < plan.owners)
    def _():
        mine = my_piece + gy * own
        pltpu.make_async_copy(
            tiles.at[pl.ds(mine, own)], y_in.at[pl.ds(gy * own, own)], rs_recv.at[chips]
        ).start()
        pltpu.make_async_copy(y_in, y_in, rs_recv.at[chips]).wait()
        for i in range(own):
            value = y_in[i]
            for source in range(1, n_gy):
                value = value + y_in[source * own + i]
            summed[mine + i] = value

        @pl.loop(1, n_gy)
        def _(step):
            to = lax.rem(gy + step, n_gy)
            remote(
                summed.at[pl.ds(mine, own)], summed.at[pl.ds(mine, own)], rs_send.at[3], e_recv.at[0], gx, to
            ).start()

    sent_own = tiles.at[pl.ds(my_piece, own)]

    @pl.loop(1, n_gy)
    def _(step):
        to = lax.rem(gy + step, n_gy)

        @pl.when(to < plan.owners)
        def _():
            pltpu.make_async_copy(sent_own, sent_own, rs_send.at[2]).wait()

    whole = summed.at[pl.ds(my_piece, piece)]
    rest = summed.at[pl.ds(my_piece, piece - own)]

    @pl.when(gy < plan.owners)
    def _():
        if plan.owners > 1:
            pltpu.make_async_copy(rest, rest, e_recv.at[0]).wait()

    @pl.when(gy >= plan.owners)
    def _():
        pltpu.make_async_copy(whole, whole, e_recv.at[0]).wait()

    gathers = []
    for step in range(1, chips):
        to = lax.rem(xi + step, chips)
        send = remote(whole, whole, rs_send.at[4], e_recv.at[step], 2 * to + core, gy)
        send.start()
        gathers.append(send)
    for send in gathers:
        send.wait_recv()
    mine_half = summed.at[pl.ds(my_half, half)]
    last = remote(mine_half, mine_half, rs_send.at[5], e_recv.at[chips], 2 * xi + 1 - core, gy)
    last.start()
    last.wait()

    for index, (row, tile) in enumerate(plan.tiles):
        width = min(LANES, n_y - tile * LANES)
        where = (slice(row, row + ROWS), slice(tile * LANES, tile * LANES + width))
        out_ref[where] = out_ref[where] + summed[index, :, 0:width]

    for send in x_sends:
        send.wait_send()
    for send in gathers:
        send.wait_send()

    @pl.when(gy < plan.owners)
    def _():
        @pl.loop(1, n_gy)
        def _(step):
            own_tiles = y_in.at[pl.ds(0, own)]
            pltpu.make_async_copy(own_tiles, own_tiles, rs_send.at[3]).wait()

    for index, (low, size) in enumerate(plan.chunks):
        there = fbuf.at[pl.ds(low, size), 0]

        @pl.loop(1, n_gx)
        def _(step):
            pltpu.make_async_copy(there, there, s1_send.at[index]).wait()

        tile_there = pbuf.at[pl.ds(low, size), 0]

        @pl.loop(1, 2 * n_gy)
        def _(step):
            pltpu.make_async_copy(tile_there, tile_there, s2_send).wait()
    if has_extra:
        there_extra = fbuf.at[pl.ds(low_extra, 1), 0]
        tile_extra = pbuf.at[pl.ds(low_extra, 1), 0]

        @pl.loop(1, chips)
        def _(step):
            pltpu.make_async_copy(there_extra, there_extra, s1_send.at[extra_slot]).wait()

        @pl.when(core == 1)
        def _():
            pltpu.make_async_copy(there_extra, there_extra, s1_send.at[extra_slot]).wait()

        @pl.when(core == 0)
        def _():
            @pl.loop(1, 2 * n_gy)
            def _(step):
                pltpu.make_async_copy(tile_extra, tile_extra, e_send).wait()


def updated_total(plan, fields, x_factor, running_r):
    by_y = jnp.transpose(fields, (1, 0, 2))
    xt = jnp.transpose(x_factor).reshape(plan.rank, plan.n_gx, plan.x_block)
    xt = jnp.pad(xt, ((0, 0), (0, 0), (0, plan.x_pad - plan.x_block))).reshape(plan.rank, plan.n_gx * plan.x_pad)
    n_y = plan.full_y
    chunks = len(plan.chunks) + 1
    vmem = pl.BlockSpec(memory_space=pltpu.VMEM)
    return pl.pallas_call(
        functools.partial(exchange_kernel, plan),
        out_shape=jax.ShapeDtypeStruct((n_y, n_y), jnp.float32),
        in_specs=[pl.BlockSpec(memory_space=pl.ANY), vmem, vmem],
        out_specs=vmem,
        scratch_shapes=[
            pltpu.VMEM((plan.y_first, plan.n_gx, plan.x_block, plan.part_cells), jnp.bfloat16),
            pltpu.VMEM((plan.n_gx * plan.x_pad, plan.part_cells), jnp.bfloat16),
            pltpu.VMEM((plan.y_first, plan.units, UNIT, LANES), jnp.bfloat16),
            pltpu.VMEM((n_y, UNIT, LANES), jnp.bfloat16),
            pltpu.VMEM((UNIT // 2, n_y, 2 * LANES), jnp.bfloat16),
            pltpu.VMEM((n_y, n_y), jnp.float32),
            pltpu.VMEM((plan.n_tiles, ROWS, LANES), jnp.float32),
            pltpu.VMEM((plan.n_tiles, ROWS, LANES), jnp.float32),
            pltpu.VMEM((plan.half, ROWS, LANES), jnp.float32),
            pltpu.VMEM((plan.chips, plan.piece, ROWS, LANES), jnp.float32),
            pltpu.VMEM((plan.n_gy * plan.per_owner, ROWS, LANES), jnp.float32),
            pltpu.SemaphoreType.DMA((chunks,)),
            pltpu.SemaphoreType.DMA((chunks, plan.n_gx)),
            pltpu.SemaphoreType.DMA,
            pltpu.SemaphoreType.DMA,
            pltpu.SemaphoreType.DMA,
            pltpu.SemaphoreType.DMA((plan.chips + 1,)),
            pltpu.SemaphoreType.DMA((6,)),
            pltpu.SemaphoreType.DMA((plan.chips + 1,)),
            pltpu.SemaphoreType.DMA,
        ],
        compiler_params=pltpu.CompilerParams(
            collective_id=0, has_side_effects=True, vmem_limit_bytes=48 * 1024 * 1024
        ),
        name="exchange",
    )(by_y, xt, running_r)


def on_device(n_gx, n_gy, fields, x_factor, running_r):
    x_block, y_block, cells = fields.shape
    full_y = running_r.shape[0]
    plan = Plan(n_gx, n_gy, x_block, y_block, cells, x_factor.shape[1], full_y)
    total = updated_total(plan, fields, x_factor, running_r)
    upper_r = lax.linalg.cholesky(total.T, symmetrize_input=False).T
    row_block = full_y // n_gy
    col_block = full_y // n_gx
    return lax.dynamic_slice(
        upper_r,
        (lax.axis_index("gy") * row_block, lax.axis_index("gx") * col_block),
        (row_block, col_block),
    )


def solution(mesh):
    in_specs = (P("gx", "gy", None), P(), P())
    out_specs = P("gy", "gx")
    return jax.shard_map(
        functools.partial(on_device, mesh.shape["gx"], mesh.shape["gy"]),
        mesh=mesh, in_specs=in_specs, out_specs=out_specs, check_vma=False,
    )
```

```python
import functools

import jax
import jax.numpy as jnp
from jax import lax
from jax.experimental import pallas as pl
from jax.experimental.pallas import tpu as pltpu
from jax.sharding import PartitionSpec as P

MESH = pl.DeviceIdType.MESH
LANES = 128
ROWS = 8
UNIT = 16
HIGH = lax.Precision.HIGHEST


def round_up(value, step):
    return -(-value // step) * step


class Plan:
    def __init__(self, n_gx, n_gy, x_block, y_block, cells, rank, full_y):
        self.n_gx, self.n_gy = n_gx, n_gy
        self.chips = n_gx // 2
        self.x_block = x_block
        self.x_pad = round_up(x_block, 32)
        self.y_block = y_block
        self.y_first = (y_block + 1) // 2
        self.y_common = y_block // 2
        self.cell_tiles = cells // LANES // self.chips
        self.part_cells = self.cell_tiles * LANES
        self.rank = rank
        self.rank_units = rank // UNIT
        self.units = self.cell_tiles * self.rank_units
        self.full_y = full_y
        self.y_lanes = round_up(full_y, LANES)
        self.chunks = self.make_chunks()
        tiles = []
        for row in range(0, full_y, ROWS):
            for tile in range(row // LANES, self.y_lanes // LANES):
                tiles.append((row, tile))
        self.tiles = tiles
        owners = min(n_gy, -(-len(tiles) // (2 * n_gx)))
        self.per_owner = -(-len(tiles) // (n_gx * owners))
        self.owners = -(-len(tiles) // (n_gx * self.per_owner))
        self.piece = self.per_owner * self.owners
        self.half = self.piece * self.chips
        self.n_tiles = 2 * self.half

    def make_chunks(self):
        count = min(5, self.y_common)
        bounds = [self.y_common * i // count for i in range(count + 1)]
        return [(low, high - low) for low, high in zip(bounds[:-1], bounds[1:])]


def exchange_kernel(
    plan, f_hbm, xt_ref, r_ref, out_ref,
    fbuf, fibres, pbuf, gbuf, mbuf, gram, tiles, summed, core_in, x_in, y_in,
    s1_send, s1_recv, s2_send, s2_recv, e_send, e_recv, rs_send, rs_recv, loc,
):
    n_gx, n_gy, chips = plan.n_gx, plan.n_gy, plan.chips
    gx = lax.axis_index("gx")
    gy = lax.axis_index("gy")
    xi = gx // 2
    core = gx % 2
    units = plan.units
    has_extra = plan.y_first > plan.y_common
    extra_slot = len(plan.chunks)

    def remote(src, dst, send, recv, to_gx, to_gy):
        return pltpu.make_async_remote_copy(
            src_ref=src, dst_ref=dst, send_sem=send, recv_sem=recv,
            device_id=(to_gx, to_gy), device_id_type=MESH,
        )

    barrier = pltpu.get_barrier_semaphore()

    @pl.loop(1, n_gx)
    def _(step):
        pl.semaphore_signal(barrier, inc=1, device_id=(lax.rem(gx + step, n_gx), gy), device_id_type=MESH)

    @pl.loop(1, n_gy)
    def _(step):
        to_gy = lax.rem(gy + step, n_gy)
        pl.semaphore_signal(barrier, inc=1, device_id=(2 * xi, to_gy), device_id_type=MESH)
        pl.semaphore_signal(barrier, inc=1, device_id=(2 * xi + 1, to_gy), device_id_type=MESH)

    if plan.x_pad > plan.x_block:
        for block in range(n_gx):
            low = block * plan.x_pad + plan.x_block
            high = (block + 1) * plan.x_pad
            fibres[low:high, :] = jnp.zeros((high - low, plan.part_cells), jnp.bfloat16)

    pl.semaphore_wait(barrier, (n_gx - 1) + 2 * (n_gy - 1))

    def field_src(to_core, to_chip, low, size):
        return f_hbm.at[
            pl.ds(plan.y_first * to_core + low, size), :,
            pl.ds(pl.multiple_of(plan.part_cells * to_chip, LANES), plan.part_cells),
        ]

    def field_dst(low, size):
        return fbuf.at[pl.ds(low, size), gx]

    def stage1(index, low, size):
        local = pltpu.make_async_copy(
            field_src(core, xi, low, size), field_dst(low, size), s1_recv.at[index, gx]
        )
        local.start()

        @pl.loop(1, n_gx)
        def _(step):
            to = lax.rem(gx + step, n_gx)
            remote(
                field_src(to % 2, to // 2, low, size), field_dst(low, size),
                s1_send.at[index], s1_recv.at[index, gx], to, gy,
            ).start()

    for index, (low, size) in enumerate(plan.chunks):
        stage1(index, low, size)
    low_extra = plan.y_common
    if has_extra:
        @pl.loop(1, chips)
        def _(step):
            to_chip = lax.rem(xi + step, chips)
            remote(
                field_src(0, to_chip, low_extra, 1), field_dst(low_extra, 1),
                s1_send.at[extra_slot], s1_recv.at[extra_slot, gx], 2 * to_chip, gy,
            ).start()

        @pl.when(core == 0)
        def _():
            pltpu.make_async_copy(
                field_src(0, xi, low_extra, 1), field_dst(low_extra, 1), s1_recv.at[extra_slot, gx]
            ).start()

        @pl.when(core == 1)
        def _():
            remote(
                field_src(0, xi, low_extra, 1), field_dst(low_extra, 1),
                s1_send.at[extra_slot], s1_recv.at[extra_slot, gx], 2 * xi, gy,
            ).start()

    def project(y):
        for block in range(n_gx):
            low = block * plan.x_pad
            fibres[low:low + plan.x_block, :] = fbuf[y, block]
        product = jnp.dot(xt_ref[...], fibres[...], preferred_element_type=jnp.float32).astype(jnp.bfloat16)
        for tile in range(plan.cell_tiles):
            part = product[:, tile * LANES:(tile + 1) * LANES]
            pbuf[y, pl.ds(tile * plan.rank_units, plan.rank_units)] = part.reshape(plan.rank_units, UNIT, LANES)

    def tile_src(unit, low, size):
        return pbuf.at[pl.ds(low, size), lax.rem(unit, units)]

    def tile_dst(low, size):
        return gbuf.at[pl.ds(plan.y_block * gy + plan.y_first * core + low, size)]

    def stage2(low, size, send, recv):
        pltpu.make_async_copy(tile_src(2 * gy + core, low, size), tile_dst(low, size), recv).start()
        remote(
            tile_src(2 * gy + 1 - core, low, size), tile_dst(low, size), send, recv, 2 * xi + 1 - core, gy
        ).start()

        @pl.loop(1, n_gy)
        def _(step):
            to_gy = lax.rem(gy + step, n_gy)
            for to_core in range(2):
                remote(
                    tile_src(2 * to_gy + to_core, low, size), tile_dst(low, size), send, recv,
                    2 * xi + to_core, to_gy,
                ).start()

    def chunk_done(index, low, size):
        for source in range(n_gx):
            there = fbuf.at[pl.ds(low, size), source]
            pltpu.make_async_copy(there, there, s1_recv.at[index, source]).wait()

    for index, (low, size) in enumerate(plan.chunks):
        chunk_done(index, low, size)

        @pl.loop(low, low + size)
        def _(y):
            project(y)

        stage2(low, size, s2_send, s2_recv)

    if has_extra:
        @pl.when(core == 0)
        def _():
            chunk_done(extra_slot, low_extra, 1)
            project(low_extra)
            stage2(low_extra, 1, e_send, s2_recv)

    n_y = plan.full_y
    for low in range(0, n_y, LANES):
        high = min(low + LANES, n_y)
        out_ref[low:high, low:n_y] = lax.dot_general(
            r_ref[0:high, low:high], r_ref[0:high, low:n_y], (((0,), (0,)), ((), ())),
            precision=HIGH, preferred_element_type=jnp.float32,
        )
        if low:
            out_ref[low:high, 0:low] = jnp.zeros((high - low, low), jnp.float32)

    size = UNIT * UNIT
    to_row = lax.broadcasted_iota(jnp.int32, (size, size), 0)
    from_row = lax.broadcasted_iota(jnp.int32, (size, size), 1)
    turn = ((to_row % UNIT == from_row // UNIT) & (to_row // UNIT == from_row % UNIT)).astype(jnp.bfloat16)

    pltpu.make_async_copy(gbuf, gbuf, s2_recv).wait()

    @pl.loop(0, n_y // UNIT)
    def _(group):
        rows = pl.ds(pl.multiple_of(group * UNIT, UNIT), UNIT)
        block = gbuf[rows].reshape(size, LANES)
        turned = jnp.dot(turn, block, preferred_element_type=jnp.float32).astype(jnp.bfloat16)
        turned = turned.reshape(UNIT, UNIT, LANES)
        for a in range(UNIT):
            mbuf[a // 2, rows, (a % 2) * LANES:(a % 2 + 1) * LANES] = turned[a]

    keep = jnp.where(2 * gy + core < units, 1.0, 0.0).astype(jnp.float32)
    for low in range(0, n_y, LANES):
        high = min(low + LANES, n_y)
        total = jnp.zeros((high - low, n_y - low), jnp.float32)
        for a in range(UNIT // 2):
            total = total + lax.dot_general(
                mbuf[a, low:high, :], mbuf[a, low:n_y, :], (((1,), (1,)), ((), ())),
                preferred_element_type=jnp.float32,
            )
        gram[low:high, low:n_y] = total * keep

    gap = plan.y_lanes - n_y
    for index, (row, tile) in enumerate(plan.tiles):
        width = min(LANES, n_y - tile * LANES)
        if width < LANES:
            tiles[index] = jnp.zeros((ROWS, LANES), jnp.float32)
        tiles[index, :, 0:width] = gram[row:row + ROWS, tile * LANES:tile * LANES + width]
    for index in range(len(plan.tiles), plan.n_tiles):
        tiles[index] = jnp.zeros((ROWS, LANES), jnp.float32)

    half, piece, own = plan.half, plan.piece, plan.per_owner
    my_half = core * half
    other_half = (1 - core) * half
    send = remote(
        tiles.at[pl.ds(other_half, half)], core_in, rs_send.at[0], rs_recv.at[0], 2 * xi + 1 - core, gy
    )
    send.start()
    send.wait()

    def add_core(i):
        tiles[my_half + i] += core_in[i]
    pl.loop(0, half)(add_core)

    x_sends = []
    for step in range(1, chips):
        to = lax.rem(xi + step, chips)
        send = remote(
            tiles.at[pl.ds(my_half + to * piece, piece)], x_in.at[step], rs_send.at[1], rs_recv.at[step],
            2 * to + core, gy,
        )
        send.start()
        x_sends.append(send)
    for send in x_sends:
        send.wait_recv()
    my_piece = my_half + xi * piece

    def add_x(i):
        value = tiles[my_piece + i]
        for step in range(1, chips):
            value = value + x_in[step, i]
        tiles[my_piece + i] = value
    pl.loop(0, piece)(add_x)

    @pl.loop(1, n_gy)
    def _(step):
        to = lax.rem(gy + step, n_gy)

        @pl.when(to < plan.owners)
        def _():
            remote(
                tiles.at[pl.ds(my_piece + to * own, own)], y_in.at[pl.ds(gy * own, own)], rs_send.at[2], rs_recv.at[chips],
                gx, to,
            ).start()

    @pl.when(gy < plan.owners)
    def _():
        mine = my_piece + gy * own
        pltpu.make_async_copy(
            tiles.at[pl.ds(mine, own)], y_in.at[pl.ds(gy * own, own)], rs_recv.at[chips]
        ).start()
        pltpu.make_async_copy(y_in, y_in, rs_recv.at[chips]).wait()
        for i in range(own):
            value = y_in[i]
            for source in range(1, n_gy):
                value = value + y_in[source * own + i]
            summed[mine + i] = value

        @pl.loop(1, n_gy)
        def _(step):
            to = lax.rem(gy + step, n_gy)
            remote(
                summed.at[pl.ds(mine, own)], summed.at[pl.ds(mine, own)], rs_send.at[3], e_recv.at[0], gx, to
            ).start()

    sent_own = tiles.at[pl.ds(my_piece, own)]

    @pl.loop(1, n_gy)
    def _(step):
        to = lax.rem(gy + step, n_gy)

        @pl.when(to < plan.owners)
        def _():
            pltpu.make_async_copy(sent_own, sent_own, rs_send.at[2]).wait()

    whole = summed.at[pl.ds(my_piece, piece)]
    rest = summed.at[pl.ds(my_piece, piece - own)]

    @pl.when(gy < plan.owners)
    def _():
        if plan.owners > 1:
            pltpu.make_async_copy(rest, rest, e_recv.at[0]).wait()

    @pl.when(gy >= plan.owners)
    def _():
        pltpu.make_async_copy(whole, whole, e_recv.at[0]).wait()

    gathers = []
    for step in range(1, chips):
        to = lax.rem(xi + step, chips)
        send = remote(whole, whole, rs_send.at[4], e_recv.at[step], 2 * to + core, gy)
        send.start()
        gathers.append(send)
    for send in gathers:
        send.wait_recv()
    mine_half = summed.at[pl.ds(my_half, half)]
    last = remote(mine_half, mine_half, rs_send.at[5], e_recv.at[chips], 2 * xi + 1 - core, gy)
    last.start()
    last.wait()

    for index, (row, tile) in enumerate(plan.tiles):
        width = min(LANES, n_y - tile * LANES)
        where = (slice(row, row + ROWS), slice(tile * LANES, tile * LANES + width))
        out_ref[where] = out_ref[where] + summed[index, :, 0:width]

    for send in x_sends:
        send.wait_send()
    for send in gathers:
        send.wait_send()

    @pl.when(gy < plan.owners)
    def _():
        @pl.loop(1, n_gy)
        def _(step):
            own_tiles = y_in.at[pl.ds(0, own)]
            pltpu.make_async_copy(own_tiles, own_tiles, rs_send.at[3]).wait()

    for index, (low, size) in enumerate(plan.chunks):
        there = fbuf.at[pl.ds(low, size), 0]

        @pl.loop(1, n_gx)
        def _(step):
            pltpu.make_async_copy(there, there, s1_send.at[index]).wait()

        tile_there = pbuf.at[pl.ds(low, size), 0]

        @pl.loop(1, 2 * n_gy)
        def _(step):
            pltpu.make_async_copy(tile_there, tile_there, s2_send).wait()
    if has_extra:
        there_extra = fbuf.at[pl.ds(low_extra, 1), 0]
        tile_extra = pbuf.at[pl.ds(low_extra, 1), 0]

        @pl.loop(1, chips)
        def _(step):
            pltpu.make_async_copy(there_extra, there_extra, s1_send.at[extra_slot]).wait()

        @pl.when(core == 1)
        def _():
            pltpu.make_async_copy(there_extra, there_extra, s1_send.at[extra_slot]).wait()

        @pl.when(core == 0)
        def _():
            @pl.loop(1, 2 * n_gy)
            def _(step):
                pltpu.make_async_copy(tile_extra, tile_extra, e_send).wait()


def updated_total(plan, fields, x_factor, running_r):
    by_y = jnp.transpose(fields, (1, 0, 2))
    xt = jnp.transpose(x_factor).reshape(plan.rank, plan.n_gx, plan.x_block)
    xt = jnp.pad(xt, ((0, 0), (0, 0), (0, plan.x_pad - plan.x_block))).reshape(plan.rank, plan.n_gx * plan.x_pad)
    n_y = plan.full_y
    chunks = len(plan.chunks) + 1
    vmem = pl.BlockSpec(memory_space=pltpu.VMEM)
    return pl.pallas_call(
        functools.partial(exchange_kernel, plan),
        out_shape=jax.ShapeDtypeStruct((n_y, n_y), jnp.float32),
        in_specs=[pl.BlockSpec(memory_space=pl.ANY), vmem, vmem],
        out_specs=vmem,
        scratch_shapes=[
            pltpu.VMEM((plan.y_first, plan.n_gx, plan.x_block, plan.part_cells), jnp.bfloat16),
            pltpu.VMEM((plan.n_gx * plan.x_pad, plan.part_cells), jnp.bfloat16),
            pltpu.VMEM((plan.y_first, plan.units, UNIT, LANES), jnp.bfloat16),
            pltpu.VMEM((n_y, UNIT, LANES), jnp.bfloat16),
            pltpu.VMEM((UNIT // 2, n_y, 2 * LANES), jnp.bfloat16),
            pltpu.VMEM((n_y, n_y), jnp.float32),
            pltpu.VMEM((plan.n_tiles, ROWS, LANES), jnp.float32),
            pltpu.VMEM((plan.n_tiles, ROWS, LANES), jnp.float32),
            pltpu.VMEM((plan.half, ROWS, LANES), jnp.float32),
            pltpu.VMEM((plan.chips, plan.piece, ROWS, LANES), jnp.float32),
            pltpu.VMEM((plan.n_gy * plan.per_owner, ROWS, LANES), jnp.float32),
            pltpu.SemaphoreType.DMA((chunks,)),
            pltpu.SemaphoreType.DMA((chunks, plan.n_gx)),
            pltpu.SemaphoreType.DMA,
            pltpu.SemaphoreType.DMA,
            pltpu.SemaphoreType.DMA,
            pltpu.SemaphoreType.DMA((plan.chips + 1,)),
            pltpu.SemaphoreType.DMA((6,)),
            pltpu.SemaphoreType.DMA((plan.chips + 1,)),
            pltpu.SemaphoreType.DMA,
        ],
        compiler_params=pltpu.CompilerParams(
            collective_id=0, has_side_effects=True, vmem_limit_bytes=48 * 1024 * 1024
        ),
        name="exchange",
    )(by_y, xt, running_r)


def element(row, lane):
    return jnp.broadcast_to(row[0:1, lane:lane + 1], (ROWS, LANES))

def factor_panel(rows, lane):
    rows = list(rows)
    diag = {(k, i): element(rows[k], lane + i) for k in range(ROWS) for i in range(k, ROWS)}
    done = []
    for k in range(ROWS):
        inv = lax.rsqrt(diag[k, k])
        scaled = {i: diag[k, i] * inv for i in range(k + 1, ROWS)}
        top = rows[k] * inv
        done.append(top)
        for i in range(k + 1, ROWS):
            for j in range(i, ROWS):
                diag[i, j] = diag[i, j] - scaled[i] * scaled[j]
            rows[i] = rows[i] - scaled[i] * top
    return done

def chol_kernel(n, a_ref, u_ref, work, rowbuf, spread):
    nb = -(-n // LANES); width = nb * LANES
    for t in range(nb):
        w = min(LANES, n - t * LANES)
        work[t, 0:n, 0:w] = a_ref[:, t * LANES:t * LANES + w]

    def block(b, panels, tiles):
        start = pl.multiple_of(b * LANES, LANES)
        for p in range(panels):
            for s in range(tiles):
                t = jnp.minimum(b + s, nb - 1)
                rowbuf[pl.ds(p * 64 + s, ROWS, stride=ROWS), :] = work[t, pl.ds(start + p * ROWS, ROWS), :]
        def get(i):
            return rowbuf[i * ROWS:(i + 1) * ROWS, :]
        def put(i, v):
            rowbuf[i * ROWS:(i + 1) * ROWS, :] = v
        rows = [get(i) for i in range(ROWS)]
        for p in range(panels):
            lane = p * ROWS
            done = factor_panel(rows, lane)
            for k in range(ROWS):
                put(lane + k, done[k])
            if p + 1 == panels:
                break
            rows = []
            for i in range(ROWS):
                value = get(lane + ROWS + i)
                acc = None
                for k in range(ROWS):
                    term = element(done[k], lane + ROWS + i) * done[k]
                    acc = term if acc is None else acc + term
                rows.append(value - acc)
            if p + 2 < panels:
                flat = rowbuf[pl.ds(lane * ROWS, ROWS, stride=ROWS), :]
                for i in range((p + 2) * ROWS, panels * ROWS):
                    spread[i * ROWS:(i + 1) * ROWS, :] = jnp.broadcast_to(flat[:, i:i + 1], (ROWS, LANES))
                    acc = None
                    for k in range(ROWS):
                        term = spread[pl.ds(i * ROWS + k, ROWS, stride=0), :] * done[k]
                        acc = term if acc is None else acc + term
                    put(i, get(i) - acc)
        for p in range(panels):
            for s in range(tiles):
                t = jnp.minimum(b + s, nb - 1)
                def move():
                    work[t, pl.ds(start + p * ROWS, ROWS), :] = rowbuf[pl.ds(p * 64 + s, ROWS, stride=ROWS), :]
                pl.when(b + s < nb)(move)

    full = n // LANES
    rest = (n - full * LANES) // ROWS
    @pl.loop(0, full)
    def _(b):
        block(b, LANES // ROWS, nb)
        for static in range(full):
            if (static + 1) * LANES < n:
                @pl.when(b == static)
                def _():
                    low = static * LANES
                    for r in range(static + 1, nb):
                        hi = min((r + 1) * LANES, n)
                        left = work[r, low:low + LANES, 0:hi - r * LANES]
                        for c in range(r, nb):
                            right = work[c, low:low + LANES, :]
                            work[c, r * LANES:hi, :] -= lax.dot_general(left, right, (((0,), (0,)), ((), ())), precision=HIGH, preferred_element_type=jnp.float32)
    if rest:
        block(full, rest, 1)
    for t in range(nb):
        w = min(LANES, n - t * LANES)
        for r in range(nb):
            hi = min((r + 1) * LANES, n); lo = r * LANES
            if r < t:
                u_ref[lo:hi, t * LANES:t * LANES + w] = work[t, lo:hi, 0:w]
            elif r > t:
                u_ref[lo:hi, t * LANES:t * LANES + w] = jnp.zeros((hi - lo, w), jnp.float32)
            else:
                v = work[t, lo:hi, 0:w]
                keep = lax.broadcasted_iota(jnp.int32, v.shape, 0) <= lax.broadcasted_iota(jnp.int32, v.shape, 1)
                u_ref[lo:hi, t * LANES:t * LANES + w] = jnp.where(keep, v, 0.0)

def upper_factor(a):
    n = a.shape[0]; nb = -(-n // LANES)
    return pl.pallas_call(
        functools.partial(chol_kernel, n),
        out_shape=jax.ShapeDtypeStruct((n, n), jnp.float32),
        in_specs=[pl.BlockSpec(memory_space=pltpu.VMEM)], out_specs=pl.BlockSpec(memory_space=pltpu.VMEM),
        scratch_shapes=[pltpu.VMEM((nb, nb * LANES, LANES), jnp.float32), pltpu.VMEM((LANES * ROWS, LANES), jnp.float32), pltpu.VMEM((LANES * ROWS, LANES), jnp.float32)],
        compiler_params=pltpu.CompilerParams(vmem_limit_bytes=40 * 1024 * 1024), name="factor",
    )(a)


def on_device(n_gx, n_gy, fields, x_factor, running_r):
    x_block, y_block, cells = fields.shape
    full_y = running_r.shape[0]
    plan = Plan(n_gx, n_gy, x_block, y_block, cells, x_factor.shape[1], full_y)
    total = updated_total(plan, fields, x_factor, running_r)
    upper_r = upper_factor(total)
    row_block = full_y // n_gy
    col_block = full_y // n_gx
    return lax.dynamic_slice(
        upper_r,
        (lax.axis_index("gy") * row_block, lax.axis_index("gx") * col_block),
        (row_block, col_block),
    )


def solution(mesh):
    in_specs = (P("gx", "gy", None), P(), P())
    out_specs = P("gy", "gx")
    return jax.shard_map(
        functools.partial(on_device, mesh.shape["gx"], mesh.shape["gy"]),
        mesh=mesh, in_specs=in_specs, out_specs=out_specs, check_vma=False,
    )
```

```python
import functools

import jax
import jax.numpy as jnp
from jax import lax
from jax.experimental import pallas as pl
from jax.experimental.pallas import tpu as pltpu
from jax.sharding import PartitionSpec as P

MESH = pl.DeviceIdType.MESH
LANES = 128
ROWS = 8
UNIT = 16
NARROW = 32
HIGH = lax.Precision.HIGHEST


def round_up(value, step):
    return -(-value // step) * step


def ring_offsets(size, distance):
    if distance >= size:
        return []
    return [distance] if 2 * distance == size else [distance, size - distance]


def doublings(size):
    distance = 1
    while distance < size:
        yield distance
        distance *= 2


class Plan:
    def __init__(self, n_gx, n_gy, x_block, y_block, cells, rank, full_y):
        self.n_gx, self.n_gy = n_gx, n_gy
        self.chips = n_gx // 2
        self.n_z = 8 if n_gy % 8 == 0 else n_gy
        self.n_yy = n_gy // self.n_z
        self.x_block = x_block
        self.x_pad = round_up(x_block, 32)
        self.y_block = y_block
        self.y_first = (y_block + 1) // 2
        self.y_common = y_block // 2
        self.cell_tiles = cells // LANES // self.chips
        self.part_cells = self.cell_tiles * LANES
        self.rank = rank
        self.rank_units = rank // UNIT
        self.units = self.cell_tiles * self.rank_units
        self.full_y = full_y
        self.chunks = self.make_chunks()
        self.pieces, used = self.pack()
        self.slots = self.n_z // 2
        self.per_owner = -(-used // (n_gx * n_gy))
        self.part = self.chips * self.n_yy * self.slots * self.per_owner
        self.half = 2 * self.part
        self.n_tiles = 2 * self.half

    def pack(self):
        pieces, narrow, used = [], [], 0
        for row in range(0, self.full_y, ROWS):
            for start in range(row // LANES * LANES, self.full_y, LANES):
                low = max(row, start) // NARROW * NARROW
                high = min(start + LANES, self.full_y)
                if high - low <= NARROW:
                    narrow.append((row, low, high - low))
                else:
                    pieces.append((row, start, high - start, used, 0))
                    used += 1
        for index, (row, low, width) in enumerate(narrow):
            share = LANES // NARROW
            pieces.append((row, low, width, used + index // share, index % share * NARROW))
        return pieces, used + -(-len(narrow) * NARROW // LANES)

    def make_chunks(self):
        sizes = []
        left = self.y_common
        while left:
            size = 1 if len(sizes) < 2 else 2
            sizes.append(min(size, left))
            left -= sizes[-1]
        chunks, low = [], 0
        for size in sizes:
            chunks.append((low, size))
            low += size
        return chunks


def exchange_kernel(
    plan, f_hbm, x_hbm, r_hbm, out_ref,
    fbuf, fibres, x_rows, x_pad, xt_ref, r_ref, pbuf, gbuf, mbuf, gram, tiles, summed, core_in, axis_in, z_in,
    s1_send, s1_recv, s2_send, s2_recv, e_send, rs_send, rs_recv, loc, hands,
):
    n_gx, n_gy, chips = plan.n_gx, plan.n_gy, plan.chips
    gx = lax.axis_index("gx")
    gy = lax.axis_index("gy")
    xi = gx // 2
    core = gx % 2
    units = plan.units
    has_extra = plan.y_first > plan.y_common
    extra_slot = len(plan.chunks)

    def remote(src, dst, send, recv, to_gx, to_gy):
        return pltpu.make_async_remote_copy(
            src_ref=src, dst_ref=dst, send_sem=send, recv_sem=recv,
            device_id=(to_gx, to_gy), device_id_type=MESH,
        )

    def other_gy(step_y, step_z):
        n_z, n_yy = plan.n_z, plan.n_yy
        return n_z * lax.rem(gy // n_z + step_y, n_yy) + lax.rem(gy % n_z + step_z, n_z)

    barrier = pltpu.get_barrier_semaphore()
    near = [other_gy(0, step) for step in ring_offsets(plan.n_z, 1)]
    near += [other_gy(step, 0) for step in ring_offsets(plan.n_yy, 1)]
    for to_gy in near:
        pl.semaphore_signal(barrier, inc=1, device_id=(gx, to_gy), device_id_type=MESH)
    for step in range(1, n_gx):
        pl.semaphore_signal(barrier, inc=1, device_id=(lax.rem(gx + step, n_gx), gy), device_id_type=MESH)
    fetch_x = pltpu.make_async_copy(x_hbm, x_rows, loc.at[0])
    fetch_x.start()
    fetch_r = pltpu.make_async_copy(r_hbm, r_ref, loc.at[1])
    fetch_r.start()

    if plan.x_pad > plan.x_block:
        for block in range(n_gx):
            low = block * plan.x_pad + plan.x_block
            high = (block + 1) * plan.x_pad
            fibres[low:high, :] = jnp.zeros((high - low, plan.part_cells), jnp.bfloat16)

    pl.semaphore_wait(barrier, (n_gx - 1) + len(near))

    def field_src(to_core, to_chip, low, size):
        return f_hbm.at[
            pl.ds(plan.y_first * to_core + low, size), :,
            pl.ds(pl.multiple_of(plan.part_cells * to_chip, LANES), plan.part_cells),
        ]

    def field_dst(low, size):
        return fbuf.at[pl.ds(low, size), gx]

    def stage1(index, low, size):
        local = pltpu.make_async_copy(
            field_src(core, xi, low, size), field_dst(low, size), s1_recv.at[index, gx]
        )
        local.start()

        @pl.loop(1, n_gx)
        def _(step):
            to = lax.rem(gx + step, n_gx)
            remote(
                field_src(to % 2, to // 2, low, size), field_dst(low, size),
                s1_send.at[index], s1_recv.at[index, gx], to, gy,
            ).start()

    low_extra = plan.y_common
    if has_extra:
        @pl.loop(1, chips)
        def _(step):
            to_chip = lax.rem(xi + step, chips)
            remote(
                field_src(0, to_chip, low_extra, 1), field_dst(low_extra, 1),
                s1_send.at[extra_slot], s1_recv.at[extra_slot, gx], 2 * to_chip, gy,
            ).start()

        @pl.when(core == 0)
        def _():
            pltpu.make_async_copy(
                field_src(0, xi, low_extra, 1), field_dst(low_extra, 1), s1_recv.at[extra_slot, gx]
            ).start()

        @pl.when(core == 1)
        def _():
            remote(
                field_src(0, xi, low_extra, 1), field_dst(low_extra, 1),
                s1_send.at[extra_slot], s1_recv.at[extra_slot, gx], 2 * xi, gy,
            ).start()
    for index, (low, size) in enumerate(plan.chunks):
        stage1(index, low, size)

    rounds = [(0, distance) for distance in doublings(plan.n_z)] + [(distance, 0) for distance in doublings(plan.n_yy)]
    for index, (step_y, step_z) in enumerate(rounds):
        steps = ring_offsets(plan.n_z, step_z) if step_z else ring_offsets(plan.n_yy, step_y)
        for step in steps:
            to_gy = other_gy(0, step) if step_z else other_gy(step, 0)
            pl.semaphore_signal(hands.at[index], inc=1, device_id=(gx, to_gy), device_id_type=MESH)
        pl.semaphore_wait(hands.at[index], len(steps))

    fetch_x.wait()
    x_pad[...] = jnp.zeros_like(x_pad)
    for block in range(n_gx):
        x_pad[block * plan.x_pad:block * plan.x_pad + plan.x_block, :] = x_rows[
            block * plan.x_block:(block + 1) * plan.x_block, :
        ]
    unit_row = lax.broadcasted_iota(jnp.int32, (plan.rank, plan.rank), 0)
    unit_col = lax.broadcasted_iota(jnp.int32, (plan.rank, plan.rank), 1)
    xt_ref[...] = lax.dot_general(
        (unit_row == unit_col).astype(jnp.bfloat16), x_pad[...], (((1,), (1,)), ((), ())),
        preferred_element_type=jnp.float32,
    ).astype(jnp.bfloat16)

    n_y = plan.full_y

    def square_r():
        fetch_r.wait()
        for low in range(0, n_y, LANES):
            high = min(low + LANES, n_y)
            out_ref[low:high, low:n_y] = lax.dot_general(
                r_ref[0:high, low:high], r_ref[0:high, low:n_y], (((0,), (0,)), ((), ())),
                precision=HIGH, preferred_element_type=jnp.float32,
            )
            if low:
                out_ref[low:high, 0:low] = jnp.zeros((high - low, low), jnp.float32)

    def project(y):
        for block in range(n_gx):
            low = block * plan.x_pad
            fibres[low:low + plan.x_block, :] = fbuf[y, block]
        product = jnp.dot(xt_ref[...], fibres[...], preferred_element_type=jnp.float32).astype(jnp.bfloat16)
        for tile in range(plan.cell_tiles):
            part = product[:, tile * LANES:(tile + 1) * LANES]
            pbuf[y, pl.ds(tile * plan.rank_units, plan.rank_units)] = part.reshape(plan.rank_units, UNIT, LANES)

    def tile_src(unit, low, size):
        return pbuf.at[pl.ds(low, size), lax.rem(unit, units)]

    def tile_dst(low, size):
        return gbuf.at[pl.ds(plan.y_block * gy + plan.y_first * core + low, size)]

    def stage2(low, size, send, recv):
        pltpu.make_async_copy(tile_src(2 * gy + core, low, size), tile_dst(low, size), recv).start()
        remote(
            tile_src(2 * gy + 1 - core, low, size), tile_dst(low, size), send, recv, 2 * xi + 1 - core, gy
        ).start()

        @pl.loop(1, n_gy)
        def _(step):
            to_gy = other_gy(step + step // plan.n_z, 3 * step)
            for to_core in range(2):
                remote(
                    tile_src(2 * to_gy + to_core, low, size), tile_dst(low, size), send, recv,
                    2 * xi + to_core, to_gy,
                ).start()

    def chunk_done(index, low, size):
        for source in range(n_gx):
            there = fbuf.at[pl.ds(low, size), source]
            pltpu.make_async_copy(there, there, s1_recv.at[index, source]).wait()

    if has_extra:
        @pl.when(core == 0)
        def _():
            chunk_done(extra_slot, low_extra, 1)
            project(low_extra)
            stage2(low_extra, 1, e_send, s2_recv)

    for index, (low, size) in enumerate(plan.chunks):
        chunk_done(index, low, size)

        @pl.loop(low, low + size)
        def _(y):
            project(y)

        stage2(low, size, s2_send, s2_recv)
        if index == min(2, len(plan.chunks) - 1):
            square_r()

    size = UNIT * UNIT
    to_row = lax.broadcasted_iota(jnp.int32, (size, size), 0)
    from_row = lax.broadcasted_iota(jnp.int32, (size, size), 1)
    turn = ((to_row % UNIT == from_row // UNIT) & (to_row // UNIT == from_row % UNIT)).astype(jnp.bfloat16)

    pltpu.make_async_copy(gbuf, gbuf, s2_recv).wait()

    def turn_groups(group, count):
        rows = [pl.ds(pl.multiple_of((group + i) * UNIT, UNIT), UNIT) for i in range(count)]
        blocks = [gbuf[where].reshape(size, LANES) for where in rows]
        both = blocks[0] if count == 1 else jnp.concatenate(blocks, axis=1)
        turned = jnp.dot(turn, both, preferred_element_type=jnp.float32).astype(jnp.bfloat16)
        turned = turned.reshape(UNIT, UNIT, count * LANES)
        for i in range(count):
            for a in range(UNIT):
                mbuf[rows[i], a * LANES:(a + 1) * LANES] = turned[a, :, i * LANES:(i + 1) * LANES]

    groups = n_y // UNIT
    pl.loop(0, groups // 2)(lambda pair: turn_groups(2 * pair, 2))
    if groups % 2:
        turn_groups(groups - 1, 1)

    keep = jnp.where(2 * gy + core < units, 1.0, 0.0).astype(jnp.float32)
    for low in range(0, n_y, LANES):
        high = min(low + LANES, n_y)
        gram[low:high, low:n_y] = keep * lax.dot_general(
            mbuf[low:high, :], mbuf[low:n_y, :], (((1,), (1,)), ((), ())), preferred_element_type=jnp.float32
        )

    @pl.loop(0, plan.n_tiles)
    def _(i):
        tiles[i] = jnp.zeros((ROWS, LANES), jnp.float32)

    for row, column, width, tile, lane in plan.pieces:
        tiles[tile, :, lane:lane + width] = gram[row:row + ROWS, column:column + width]

    own, slots = plan.per_owner, plan.slots
    yi, zi = gy // plan.n_z, gy % plan.n_z
    half_low = core * plan.half
    other_low = (1 - core) * plan.half
    sibling = 2 * xi + 1 - core
    started = []

    def send(src, dst, send_sem, recv_sem, to_gx, to_gy):
        copy = remote(src, dst, send_sem, recv_sem, to_gx, to_gy)
        copy.start()
        started.append(copy)
        return copy

    def along(axis, step):
        if axis == 0:
            to = lax.rem(xi + step, chips)
            return to, 2 * to + core, gy
        to = lax.rem(yi + step, plan.n_yy)
        return to, gx, plan.n_z * to + zi

    def span(tile, count):
        return pl.ds(tile, count)

    places = (xi, yi)
    counts = (chips, plan.n_yy)
    send(tiles.at[span(other_low, plan.half)], core_in, rs_send.at[0, 0], rs_recv.at[0, 0], sibling, gy).wait_recv()

    @pl.loop(0, plan.half)
    def _(i):
        tiles[half_low + i] = tiles[half_low + i] + core_in[i]

    lows = [half_low, half_low + plan.part]
    for phase in range(2):
        waits = []
        sizes = [plan.part // chips, plan.part // plan.n_yy] if phase == 0 else [slots * own] * 2
        for part in range(2):
            axis = part if phase == 0 else 1 - part
            for step in range(1, counts[axis]):
                to, to_gx, to_gy = along(axis, step)
                waits.append(send(
                    tiles.at[span(lows[part] + to * sizes[part], sizes[part])],
                    axis_in.at[2 * phase + part, step, span(0, sizes[part])],
                    rs_send.at[1 + 2 * phase + part, step], rs_recv.at[1 + 2 * phase + part, step], to_gx, to_gy,
                ))
        for copy in waits:
            copy.wait_recv()
        for part in range(2):
            axis = part if phase == 0 else 1 - part
            lows[part] = lows[part] + places[axis] * sizes[part]

            def add(i):
                value = tiles[lows[part] + i]
                for step in range(1, counts[axis]):
                    value = value + axis_in[2 * phase + part, step, i]
                tiles[lows[part] + i] = value
            pl.loop(0, sizes[part])(add)

    def slot_tile(z):
        return jnp.where(z < slots, lows[0] + z * own, lows[1] + (z - slots) * own)

    waits = []
    for step in range(1, plan.n_z):
        to = lax.rem(zi + step, plan.n_z)
        waits.append(send(
            tiles.at[span(slot_tile(to), own)], z_in.at[step], rs_send.at[5, step], rs_recv.at[5, step],
            gx, plan.n_z * yi + to,
        ))
    for copy in waits:
        copy.wait_recv()
    mine = slot_tile(zi)
    for i in range(own):
        value = tiles[mine + i]
        for step in range(1, plan.n_z):
            value = value + z_in[step, i]
        summed[mine + i] = value

    waits = []
    for step in range(1, plan.n_z):
        to = lax.rem(zi + step, plan.n_z)
        here = summed.at[span(mine, own)]
        waits.append(send(here, here, rs_send.at[6, step], rs_recv.at[6, step], gx, plan.n_z * yi + to))
    for copy in waits:
        copy.wait_recv()
    for phase in (1, 0):
        waits = []
        for part in range(2):
            axis = part if phase == 0 else 1 - part
            count = slots * own if phase == 1 else plan.part // counts[part]
            low = lows[part] if phase == 1 else half_low + part * plan.part + places[part] * count
            here = summed.at[span(low, count)]
            for step in range(1, counts[axis]):
                _, to_gx, to_gy = along(axis, step)
                waits.append(send(
                    here, here, rs_send.at[7 + 2 * phase + part, step], rs_recv.at[7 + 2 * phase + part, step], to_gx, to_gy
                ))
        for copy in waits:
            copy.wait_recv()
    here = summed.at[span(half_low, plan.half)]
    send(here, here, rs_send.at[0, 1], rs_recv.at[0, 1], sibling, gy).wait_recv()

    for row, column, width, tile, lane in plan.pieces:
        where = (slice(row, row + ROWS), slice(column, column + width))
        out_ref[where] = out_ref[where] + summed[tile, :, lane:lane + width]

    for copy in started:
        copy.wait_send()

    for index, (low, size) in enumerate(plan.chunks):
        there = fbuf.at[pl.ds(low, size), 0]

        @pl.loop(1, n_gx)
        def _(step):
            pltpu.make_async_copy(there, there, s1_send.at[index]).wait()

        tile_there = pbuf.at[pl.ds(low, size), 0]

        @pl.loop(1, 2 * n_gy)
        def _(step):
            pltpu.make_async_copy(tile_there, tile_there, s2_send).wait()
    if has_extra:
        there_extra = fbuf.at[pl.ds(low_extra, 1), 0]
        tile_extra = pbuf.at[pl.ds(low_extra, 1), 0]

        @pl.loop(1, chips)
        def _(step):
            pltpu.make_async_copy(there_extra, there_extra, s1_send.at[extra_slot]).wait()

        @pl.when(core == 1)
        def _():
            pltpu.make_async_copy(there_extra, there_extra, s1_send.at[extra_slot]).wait()

        @pl.when(core == 0)
        def _():
            @pl.loop(1, 2 * n_gy)
            def _(step):
                pltpu.make_async_copy(tile_extra, tile_extra, e_send).wait()


def updated_total(plan, fields, x_factor, running_r):
    by_y = jnp.transpose(fields, (1, 0, 2))
    n_y = plan.full_y
    chunks = len(plan.chunks) + 1
    vmem = pl.BlockSpec(memory_space=pltpu.VMEM)
    return pl.pallas_call(
        functools.partial(exchange_kernel, plan),
        out_shape=jax.ShapeDtypeStruct((n_y, n_y), jnp.float32),
        in_specs=[pl.BlockSpec(memory_space=pl.ANY)] * 3,
        out_specs=vmem,
        scratch_shapes=[
            pltpu.VMEM((plan.y_first, plan.n_gx, plan.x_block, plan.part_cells), jnp.bfloat16),
            pltpu.VMEM((plan.n_gx * plan.x_pad, plan.part_cells), jnp.bfloat16),
            pltpu.VMEM(x_factor.shape, jnp.bfloat16),
            pltpu.VMEM((plan.n_gx * plan.x_pad, plan.rank), jnp.bfloat16),
            pltpu.VMEM((plan.rank, plan.n_gx * plan.x_pad), jnp.bfloat16),
            pltpu.VMEM((n_y, n_y), jnp.float32),
            pltpu.VMEM((plan.y_first, plan.units, UNIT, LANES), jnp.bfloat16),
            pltpu.VMEM((n_y, UNIT, LANES), jnp.bfloat16),
            pltpu.VMEM((n_y, UNIT * LANES), jnp.bfloat16),
            pltpu.VMEM((n_y, n_y), jnp.float32),
            pltpu.VMEM((plan.n_tiles, ROWS, LANES), jnp.float32),
            pltpu.VMEM((plan.n_tiles, ROWS, LANES), jnp.float32),
            pltpu.VMEM((plan.half, ROWS, LANES), jnp.float32),
            pltpu.VMEM((4, max(plan.chips, plan.n_yy), plan.part // min(plan.chips, plan.n_yy), ROWS, LANES), jnp.float32),
            pltpu.VMEM((plan.n_z, plan.per_owner, ROWS, LANES), jnp.float32),
            pltpu.SemaphoreType.DMA((chunks,)),
            pltpu.SemaphoreType.DMA((chunks, plan.n_gx)),
            pltpu.SemaphoreType.DMA,
            pltpu.SemaphoreType.DMA,
            pltpu.SemaphoreType.DMA,
            pltpu.SemaphoreType.DMA((11, 8)),
            pltpu.SemaphoreType.DMA((11, 8)),
            pltpu.SemaphoreType.DMA((2,)),
            pltpu.SemaphoreType.REGULAR((8,)),
        ],
        compiler_params=pltpu.CompilerParams(
            collective_id=0, has_side_effects=True, vmem_limit_bytes=60 * 1024 * 1024
        ),
        name="exchange",
    )(by_y, x_factor, running_r)


def element(row, lane):
    return jnp.broadcast_to(row[0:1, lane:lane + 1], (ROWS, LANES))

def factor_panel(rows, lane):
    rows = list(rows)
    diag = {(k, i): element(rows[k], lane + i) for k in range(ROWS) for i in range(k, ROWS)}
    done = []
    for k in range(ROWS):
        inv = lax.rsqrt(diag[k, k])
        scaled = {i: diag[k, i] * inv for i in range(k + 1, ROWS)}
        top = rows[k] * inv
        done.append(top)
        for i in range(k + 1, ROWS):
            for j in range(i, ROWS):
                diag[i, j] = diag[i, j] - scaled[i] * scaled[j]
            rows[i] = rows[i] - scaled[i] * top
    return done

def chol_kernel(n, a_ref, u_ref, work, rowbuf, spread):
    nb = -(-n // LANES); width = nb * LANES
    for t in range(nb):
        w = min(LANES, n - t * LANES)
        work[t, 0:n, 0:w] = a_ref[:, t * LANES:t * LANES + w]

    def block(b, panels, tiles):
        start = pl.multiple_of(b * LANES, LANES)
        for p in range(panels):
            for s in range(tiles):
                t = jnp.minimum(b + s, nb - 1)
                rowbuf[pl.ds(p * 64 + s, ROWS, stride=ROWS), :] = work[t, pl.ds(start + p * ROWS, ROWS), :]
        def get(i):
            return rowbuf[i * ROWS:(i + 1) * ROWS, :]
        def put(i, v):
            rowbuf[i * ROWS:(i + 1) * ROWS, :] = v
        rows = [get(i) for i in range(ROWS)]
        for p in range(panels):
            lane = p * ROWS
            done = factor_panel(rows, lane)
            for k in range(ROWS):
                put(lane + k, done[k])
            if p + 1 == panels:
                break
            rows = []
            for i in range(ROWS):
                value = get(lane + ROWS + i)
                acc = None
                for k in range(ROWS):
                    term = element(done[k], lane + ROWS + i) * done[k]
                    acc = term if acc is None else acc + term
                rows.append(value - acc)
            if p + 2 < panels:
                flat = rowbuf[pl.ds(lane * ROWS, ROWS, stride=ROWS), :]
                for i in range((p + 2) * ROWS, panels * ROWS):
                    spread[i * ROWS:(i + 1) * ROWS, :] = jnp.broadcast_to(flat[:, i:i + 1], (ROWS, LANES))
                    acc = None
                    for k in range(ROWS):
                        term = spread[pl.ds(i * ROWS + k, ROWS, stride=0), :] * done[k]
                        acc = term if acc is None else acc + term
                    put(i, get(i) - acc)
        for p in range(panels):
            for s in range(tiles):
                t = jnp.minimum(b + s, nb - 1)
                def move():
                    work[t, pl.ds(start + p * ROWS, ROWS), :] = rowbuf[pl.ds(p * 64 + s, ROWS, stride=ROWS), :]
                pl.when(b + s < nb)(move)

    full = n // LANES
    rest = (n - full * LANES) // ROWS
    @pl.loop(0, full)
    def _(b):
        block(b, LANES // ROWS, nb)
        for static in range(full):
            if (static + 1) * LANES < n:
                @pl.when(b == static)
                def _():
                    low = static * LANES
                    for r in range(static + 1, nb):
                        hi = min((r + 1) * LANES, n)
                        left = work[r, low:low + LANES, 0:hi - r * LANES]
                        for c in range(r, nb):
                            right = work[c, low:low + LANES, :]
                            work[c, r * LANES:hi, :] -= lax.dot_general(left, right, (((0,), (0,)), ((), ())), precision=HIGH, preferred_element_type=jnp.float32)
    if rest:
        block(full, rest, 1)
    for t in range(nb):
        w = min(LANES, n - t * LANES)
        for r in range(nb):
            hi = min((r + 1) * LANES, n); lo = r * LANES
            if r < t:
                u_ref[lo:hi, t * LANES:t * LANES + w] = work[t, lo:hi, 0:w]
            elif r > t:
                u_ref[lo:hi, t * LANES:t * LANES + w] = jnp.zeros((hi - lo, w), jnp.float32)
            else:
                v = work[t, lo:hi, 0:w]
                keep = lax.broadcasted_iota(jnp.int32, v.shape, 0) <= lax.broadcasted_iota(jnp.int32, v.shape, 1)
                u_ref[lo:hi, t * LANES:t * LANES + w] = jnp.where(keep, v, 0.0)

def upper_factor(a):
    n = a.shape[0]; nb = -(-n // LANES)
    return pl.pallas_call(
        functools.partial(chol_kernel, n),
        out_shape=jax.ShapeDtypeStruct((n, n), jnp.float32),
        in_specs=[pl.BlockSpec(memory_space=pltpu.VMEM)], out_specs=pl.BlockSpec(memory_space=pltpu.VMEM),
        scratch_shapes=[pltpu.VMEM((nb, nb * LANES, LANES), jnp.float32), pltpu.VMEM((LANES * ROWS, LANES), jnp.float32), pltpu.VMEM((LANES * ROWS, LANES), jnp.float32)],
        compiler_params=pltpu.CompilerParams(vmem_limit_bytes=40 * 1024 * 1024), name="factor",
    )(a)


def on_device(n_gx, n_gy, fields, x_factor, running_r):
    x_block, y_block, cells = fields.shape
    full_y = running_r.shape[0]
    plan = Plan(n_gx, n_gy, x_block, y_block, cells, x_factor.shape[1], full_y)
    total = updated_total(plan, fields, x_factor, running_r)
    upper_r = upper_factor(total)
    row_block = full_y // n_gy
    col_block = full_y // n_gx
    return lax.dynamic_slice(
        upper_r,
        (lax.axis_index("gy") * row_block, lax.axis_index("gx") * col_block),
        (row_block, col_block),
    )


def solution(mesh):
    in_specs = (P("gx", "gy", None), P(), P())
    out_specs = P("gy", "gx")
    return jax.shard_map(
        functools.partial(on_device, mesh.shape["gx"], mesh.shape["gy"]),
        mesh=mesh, in_specs=in_specs, out_specs=out_specs, check_vma=False,
    )
```

```python
import functools

import jax
import jax.numpy as jnp
from jax import lax
from jax.experimental import pallas as pl
from jax.experimental.pallas import tpu as pltpu
from jax.sharding import PartitionSpec as P

MESH = pl.DeviceIdType.MESH
LANES = 128
ROWS = 8
UNIT = 16
NARROW = 32
HIGH = lax.Precision.HIGHEST


def round_up(value, step):
    return -(-value // step) * step


def ring_offsets(size, distance):
    if distance >= size:
        return []
    return [distance] if 2 * distance == size else [distance, size - distance]


def doublings(size):
    distance = 1
    while distance < size:
        yield distance
        distance *= 2


class Plan:
    def __init__(self, n_gx, n_gy, x_block, y_block, cells, rank, full_y):
        self.n_gx, self.n_gy = n_gx, n_gy
        self.chips = n_gx // 2
        self.n_z = 8 if n_gy % 8 == 0 else n_gy
        self.n_yy = n_gy // self.n_z
        self.x_block = x_block
        self.x_pad = round_up(x_block, 32)
        self.y_block = y_block
        self.y_first = (y_block + 1) // 2
        self.y_common = y_block // 2
        self.cell_tiles = cells // LANES // self.chips
        self.part_cells = self.cell_tiles * LANES
        self.rank = rank
        self.rank_units = rank // UNIT
        self.units = self.cell_tiles * self.rank_units
        self.full_y = full_y
        self.chunks = self.make_chunks()
        self.pieces, used = self.pack()
        self.slots = self.n_z // 2
        self.per_owner = -(-used // (n_gx * n_gy))
        self.part = self.chips * self.n_yy * self.slots * self.per_owner
        self.half = 2 * self.part
        self.n_tiles = 2 * self.half

    def pack(self):
        pieces, narrow, used = [], [], 0
        for row in range(0, self.full_y, ROWS):
            for start in range(row // LANES * LANES, self.full_y, LANES):
                low = max(row, start) // NARROW * NARROW
                high = min(start + LANES, self.full_y)
                if high - low <= NARROW:
                    narrow.append((row, low, high - low))
                else:
                    pieces.append((row, start, high - start, used, 0))
                    used += 1
        for index, (row, low, width) in enumerate(narrow):
            share = LANES // NARROW
            pieces.append((row, low, width, used + index // share, index % share * NARROW))
        return pieces, used + -(-len(narrow) * NARROW // LANES)

    def make_chunks(self):
        sizes = []
        left = self.y_common
        while left:
            size = 1
            sizes.append(min(size, left))
            left -= sizes[-1]
        chunks, low = [], 0
        for size in sizes:
            chunks.append((low, size))
            low += size
        return chunks


def exchange_kernel(
    plan, f_hbm, x_hbm, r_hbm, out_ref,
    fbuf, fibres, x_rows, x_pad, xt_ref, r_ref, pbuf, gbuf, mbuf, gram, tiles, summed, core_in, axis_in, z_in,
    s1_send, s1_recv, s2_send, s2_recv, e_send, rs_send, rs_recv, loc, hands,
):
    n_gx, n_gy, chips = plan.n_gx, plan.n_gy, plan.chips
    gx = lax.axis_index("gx")
    gy = lax.axis_index("gy")
    xi = gx // 2
    core = gx % 2
    units = plan.units
    has_extra = plan.y_first > plan.y_common
    extra_slot = len(plan.chunks)

    def remote(src, dst, send, recv, to_gx, to_gy):
        return pltpu.make_async_remote_copy(
            src_ref=src, dst_ref=dst, send_sem=send, recv_sem=recv,
            device_id=(to_gx, to_gy), device_id_type=MESH,
        )

    def other_gy(step_y, step_z):
        n_z, n_yy = plan.n_z, plan.n_yy
        return n_z * lax.rem(gy // n_z + step_y, n_yy) + lax.rem(gy % n_z + step_z, n_z)

    barrier = pltpu.get_barrier_semaphore()
    near = [other_gy(0, step) for step in ring_offsets(plan.n_z, 1)]
    near += [other_gy(step, 0) for step in ring_offsets(plan.n_yy, 1)]
    for to_gy in near:
        pl.semaphore_signal(barrier, inc=1, device_id=(gx, to_gy), device_id_type=MESH)
    for step in range(1, n_gx):
        pl.semaphore_signal(barrier, inc=1, device_id=(lax.rem(gx + step, n_gx), gy), device_id_type=MESH)
    fetch_x = pltpu.make_async_copy(x_hbm, x_rows, loc.at[0])
    fetch_x.start()
    fetch_r = pltpu.make_async_copy(r_hbm, r_ref, loc.at[1])
    fetch_r.start()

    if plan.x_pad > plan.x_block:
        for block in range(n_gx):
            low = block * plan.x_pad + plan.x_block
            high = (block + 1) * plan.x_pad
            fibres[low:high, :] = jnp.zeros((high - low, plan.part_cells), jnp.bfloat16)

    pl.semaphore_wait(barrier, (n_gx - 1) + len(near))

    def field_src(to_core, to_chip, low, size):
        return f_hbm.at[
            pl.ds(plan.y_first * to_core + low, size), :,
            pl.ds(pl.multiple_of(plan.part_cells * to_chip, LANES), plan.part_cells),
        ]

    def field_dst(low, size):
        return fbuf.at[pl.ds(low, size), gx]

    def stage1(index, low, size):
        local = pltpu.make_async_copy(
            field_src(core, xi, low, size), field_dst(low, size), s1_recv.at[index, gx]
        )
        local.start()

        @pl.loop(1, n_gx)
        def _(step):
            to = lax.rem(gx + step, n_gx)
            remote(
                field_src(to % 2, to // 2, low, size), field_dst(low, size),
                s1_send.at[index], s1_recv.at[index, gx], to, gy,
            ).start()

    low_extra = plan.y_common
    if has_extra:
        @pl.loop(1, chips)
        def _(step):
            to_chip = lax.rem(xi + step, chips)
            remote(
                field_src(0, to_chip, low_extra, 1), field_dst(low_extra, 1),
                s1_send.at[extra_slot], s1_recv.at[extra_slot, gx], 2 * to_chip, gy,
            ).start()

        @pl.when(core == 0)
        def _():
            pltpu.make_async_copy(
                field_src(0, xi, low_extra, 1), field_dst(low_extra, 1), s1_recv.at[extra_slot, gx]
            ).start()

        @pl.when(core == 1)
        def _():
            remote(
                field_src(0, xi, low_extra, 1), field_dst(low_extra, 1),
                s1_send.at[extra_slot], s1_recv.at[extra_slot, gx], 2 * xi, gy,
            ).start()
    for index, (low, size) in enumerate(plan.chunks):
        stage1(index, low, size)

    rounds = [(0, distance) for distance in doublings(plan.n_z)] + [(distance, 0) for distance in doublings(plan.n_yy)]
    for index, (step_y, step_z) in enumerate(rounds):
        steps = ring_offsets(plan.n_z, step_z) if step_z else ring_offsets(plan.n_yy, step_y)
        for step in steps:
            to_gy = other_gy(0, step) if step_z else other_gy(step, 0)
            pl.semaphore_signal(hands.at[index], inc=1, device_id=(gx, to_gy), device_id_type=MESH)
        pl.semaphore_wait(hands.at[index], len(steps))

    fetch_x.wait()
    x_pad[...] = jnp.zeros_like(x_pad)
    for block in range(n_gx):
        x_pad[block * plan.x_pad:block * plan.x_pad + plan.x_block, :] = x_rows[
            block * plan.x_block:(block + 1) * plan.x_block, :
        ]
    unit_row = lax.broadcasted_iota(jnp.int32, (plan.rank, plan.rank), 0)
    unit_col = lax.broadcasted_iota(jnp.int32, (plan.rank, plan.rank), 1)
    xt_ref[...] = lax.dot_general(
        (unit_row == unit_col).astype(jnp.bfloat16), x_pad[...], (((1,), (1,)), ((), ())),
        preferred_element_type=jnp.float32,
    ).astype(jnp.bfloat16)

    n_y = plan.full_y

    def square_r():
        fetch_r.wait()
        for low in range(0, n_y, LANES):
            high = min(low + LANES, n_y)
            out_ref[low:high, low:n_y] = lax.dot_general(
                r_ref[0:high, low:high], r_ref[0:high, low:n_y], (((0,), (0,)), ((), ())),
                precision=HIGH, preferred_element_type=jnp.float32,
            )
            if low:
                out_ref[low:high, 0:low] = jnp.zeros((high - low, low), jnp.float32)

    def project(y):
        for block in range(n_gx):
            low = block * plan.x_pad
            fibres[low:low + plan.x_block, :] = fbuf[y, block]
        product = jnp.dot(xt_ref[...], fibres[...], preferred_element_type=jnp.float32).astype(jnp.bfloat16)
        for tile in range(plan.cell_tiles):
            part = product[:, tile * LANES:(tile + 1) * LANES]
            pbuf[y, pl.ds(tile * plan.rank_units, plan.rank_units)] = part.reshape(plan.rank_units, UNIT, LANES)

    def tile_src(unit, low, size):
        return pbuf.at[pl.ds(low, size), lax.rem(unit, units)]

    def tile_dst(low, size):
        return gbuf.at[pl.ds(plan.y_block * gy + plan.y_first * core + low, size)]

    def stage2(low, size, send, recv):
        pltpu.make_async_copy(tile_src(2 * gy + core, low, size), tile_dst(low, size), recv).start()
        remote(
            tile_src(2 * gy + 1 - core, low, size), tile_dst(low, size), send, recv, 2 * xi + 1 - core, gy
        ).start()

        @pl.loop(1, n_gy)
        def _(step):
            to_gy = other_gy(step + step // plan.n_z, 3 * step)
            for to_core in range(2):
                remote(
                    tile_src(2 * to_gy + to_core, low, size), tile_dst(low, size), send, recv,
                    2 * xi + to_core, to_gy,
                ).start()

    def chunk_done(index, low, size):
        for source in range(n_gx):
            there = fbuf.at[pl.ds(low, size), source]
            pltpu.make_async_copy(there, there, s1_recv.at[index, source]).wait()

    if has_extra:
        @pl.when(core == 0)
        def _():
            chunk_done(extra_slot, low_extra, 1)
            project(low_extra)
            stage2(low_extra, 1, e_send, s2_recv)

    for index, (low, size) in enumerate(plan.chunks):
        chunk_done(index, low, size)

        @pl.loop(low, low + size)
        def _(y):
            project(y)

        stage2(low, size, s2_send, s2_recv)
        if index == min(2, len(plan.chunks) - 1):
            square_r()

    size = UNIT * UNIT
    to_row = lax.broadcasted_iota(jnp.int32, (size, size), 0)
    from_row = lax.broadcasted_iota(jnp.int32, (size, size), 1)
    turn = ((to_row % UNIT == from_row // UNIT) & (to_row // UNIT == from_row % UNIT)).astype(jnp.bfloat16)

    pltpu.make_async_copy(gbuf, gbuf, s2_recv).wait()

    def turn_groups(group, count):
        rows = [pl.ds(pl.multiple_of((group + i) * UNIT, UNIT), UNIT) for i in range(count)]
        blocks = [gbuf[where].reshape(size, LANES) for where in rows]
        both = blocks[0] if count == 1 else jnp.concatenate(blocks, axis=1)
        turned = jnp.dot(turn, both, preferred_element_type=jnp.float32).astype(jnp.bfloat16)
        turned = turned.reshape(UNIT, UNIT, count * LANES)
        for i in range(count):
            for a in range(UNIT):
                mbuf[rows[i], a * LANES:(a + 1) * LANES] = turned[a, :, i * LANES:(i + 1) * LANES]

    groups = n_y // UNIT
    pl.loop(0, groups // 2)(lambda pair: turn_groups(2 * pair, 2))
    if groups % 2:
        turn_groups(groups - 1, 1)

    keep = jnp.where(2 * gy + core < units, 1.0, 0.0).astype(jnp.float32)
    for low in range(0, n_y, LANES):
        high = min(low + LANES, n_y)
        gram[low:high, low:n_y] = keep * lax.dot_general(
            mbuf[low:high, :], mbuf[low:n_y, :], (((1,), (1,)), ((), ())), preferred_element_type=jnp.float32
        )

    @pl.loop(0, plan.n_tiles)
    def _(i):
        tiles[i] = jnp.zeros((ROWS, LANES), jnp.float32)

    for row, column, width, tile, lane in plan.pieces:
        tiles[tile, :, lane:lane + width] = gram[row:row + ROWS, column:column + width]

    own, slots = plan.per_owner, plan.slots
    yi, zi = gy // plan.n_z, gy % plan.n_z
    half_low = core * plan.half
    other_low = (1 - core) * plan.half
    sibling = 2 * xi + 1 - core
    started = []

    def send(src, dst, send_sem, recv_sem, to_gx, to_gy):
        copy = remote(src, dst, send_sem, recv_sem, to_gx, to_gy)
        copy.start()
        started.append(copy)
        return copy

    def along(axis, step):
        if axis == 0:
            to = lax.rem(xi + step, chips)
            return to, 2 * to + core, gy
        to = lax.rem(yi + step, plan.n_yy)
        return to, gx, plan.n_z * to + zi

    def span(tile, count):
        return pl.ds(tile, count)

    places = (xi, yi)
    counts = (chips, plan.n_yy)
    send(tiles.at[span(other_low, plan.half)], core_in, rs_send.at[0, 0], rs_recv.at[0, 0], sibling, gy).wait_recv()

    @pl.loop(0, plan.half)
    def _(i):
        tiles[half_low + i] = tiles[half_low + i] + core_in[i]

    lows = [half_low, half_low + plan.part]
    for phase in range(2):
        waits = []
        sizes = [plan.part // chips, plan.part // plan.n_yy] if phase == 0 else [slots * own] * 2
        for part in range(2):
            axis = part if phase == 0 else 1 - part
            for step in range(1, counts[axis]):
                to, to_gx, to_gy = along(axis, step)
                waits.append(send(
                    tiles.at[span(lows[part] + to * sizes[part], sizes[part])],
                    axis_in.at[2 * phase + part, step, span(0, sizes[part])],
                    rs_send.at[1 + 2 * phase + part, step], rs_recv.at[1 + 2 * phase + part, step], to_gx, to_gy,
                ))
        for copy in waits:
            copy.wait_recv()
        for part in range(2):
            axis = part if phase == 0 else 1 - part
            lows[part] = lows[part] + places[axis] * sizes[part]

            def add(i):
                value = tiles[lows[part] + i]
                for step in range(1, counts[axis]):
                    value = value + axis_in[2 * phase + part, step, i]
                tiles[lows[part] + i] = value
            pl.loop(0, sizes[part])(add)

    def slot_tile(z):
        return jnp.where(z < slots, lows[0] + z * own, lows[1] + (z - slots) * own)

    waits = []
    for step in range(1, plan.n_z):
        to = lax.rem(zi + step, plan.n_z)
        waits.append(send(
            tiles.at[span(slot_tile(to), own)], z_in.at[step], rs_send.at[5, step], rs_recv.at[5, step],
            gx, plan.n_z * yi + to,
        ))
    for copy in waits:
        copy.wait_recv()
    mine = slot_tile(zi)
    for i in range(own):
        value = tiles[mine + i]
        for step in range(1, plan.n_z):
            value = value + z_in[step, i]
        summed[mine + i] = value

    waits = []
    for step in range(1, plan.n_z):
        to = lax.rem(zi + step, plan.n_z)
        here = summed.at[span(mine, own)]
        waits.append(send(here, here, rs_send.at[6, step], rs_recv.at[6, step], gx, plan.n_z * yi + to))
    for copy in waits:
        copy.wait_recv()
    for phase in (1, 0):
        waits = []
        for part in range(2):
            axis = part if phase == 0 else 1 - part
            count = slots * own if phase == 1 else plan.part // counts[part]
            low = lows[part] if phase == 1 else half_low + part * plan.part + places[part] * count
            here = summed.at[span(low, count)]
            for step in range(1, counts[axis]):
                _, to_gx, to_gy = along(axis, step)
                waits.append(send(
                    here, here, rs_send.at[7 + 2 * phase + part, step], rs_recv.at[7 + 2 * phase + part, step], to_gx, to_gy
                ))
        for copy in waits:
            copy.wait_recv()
    here = summed.at[span(half_low, plan.half)]
    send(here, here, rs_send.at[0, 1], rs_recv.at[0, 1], sibling, gy).wait_recv()

    for row, column, width, tile, lane in plan.pieces:
        where = (slice(row, row + ROWS), slice(column, column + width))
        out_ref[where] = out_ref[where] + summed[tile, :, lane:lane + width]

    for copy in started:
        copy.wait_send()

    for index, (low, size) in enumerate(plan.chunks):
        there = fbuf.at[pl.ds(low, size), 0]

        @pl.loop(1, n_gx)
        def _(step):
            pltpu.make_async_copy(there, there, s1_send.at[index]).wait()

        tile_there = pbuf.at[pl.ds(low, size), 0]

        @pl.loop(1, 2 * n_gy)
        def _(step):
            pltpu.make_async_copy(tile_there, tile_there, s2_send).wait()
    if has_extra:
        there_extra = fbuf.at[pl.ds(low_extra, 1), 0]
        tile_extra = pbuf.at[pl.ds(low_extra, 1), 0]

        @pl.loop(1, chips)
        def _(step):
            pltpu.make_async_copy(there_extra, there_extra, s1_send.at[extra_slot]).wait()

        @pl.when(core == 1)
        def _():
            pltpu.make_async_copy(there_extra, there_extra, s1_send.at[extra_slot]).wait()

        @pl.when(core == 0)
        def _():
            @pl.loop(1, 2 * n_gy)
            def _(step):
                pltpu.make_async_copy(tile_extra, tile_extra, e_send).wait()


def updated_total(plan, fields, x_factor, running_r):
    by_y = jnp.transpose(fields, (1, 0, 2))
    n_y = plan.full_y
    chunks = len(plan.chunks) + 1
    vmem = pl.BlockSpec(memory_space=pltpu.VMEM)
    return pl.pallas_call(
        functools.partial(exchange_kernel, plan),
        out_shape=jax.ShapeDtypeStruct((n_y, n_y), jnp.float32),
        in_specs=[pl.BlockSpec(memory_space=pl.ANY)] * 3,
        out_specs=vmem,
        scratch_shapes=[
            pltpu.VMEM((plan.y_first, plan.n_gx, plan.x_block, plan.part_cells), jnp.bfloat16),
            pltpu.VMEM((plan.n_gx * plan.x_pad, plan.part_cells), jnp.bfloat16),
            pltpu.VMEM(x_factor.shape, jnp.bfloat16),
            pltpu.VMEM((plan.n_gx * plan.x_pad, plan.rank), jnp.bfloat16),
            pltpu.VMEM((plan.rank, plan.n_gx * plan.x_pad), jnp.bfloat16),
            pltpu.VMEM((n_y, n_y), jnp.float32),
            pltpu.VMEM((plan.y_first, plan.units, UNIT, LANES), jnp.bfloat16),
            pltpu.VMEM((n_y, UNIT, LANES), jnp.bfloat16),
            pltpu.VMEM((n_y, UNIT * LANES), jnp.bfloat16),
            pltpu.VMEM((n_y, n_y), jnp.float32),
            pltpu.VMEM((plan.n_tiles, ROWS, LANES), jnp.float32),
            pltpu.VMEM((plan.n_tiles, ROWS, LANES), jnp.float32),
            pltpu.VMEM((plan.half, ROWS, LANES), jnp.float32),
            pltpu.VMEM((4, max(plan.chips, plan.n_yy), plan.part // min(plan.chips, plan.n_yy), ROWS, LANES), jnp.float32),
            pltpu.VMEM((plan.n_z, plan.per_owner, ROWS, LANES), jnp.float32),
            pltpu.SemaphoreType.DMA((chunks,)),
            pltpu.SemaphoreType.DMA((chunks, plan.n_gx)),
            pltpu.SemaphoreType.DMA,
            pltpu.SemaphoreType.DMA,
            pltpu.SemaphoreType.DMA,
            pltpu.SemaphoreType.DMA((11, 8)),
            pltpu.SemaphoreType.DMA((11, 8)),
            pltpu.SemaphoreType.DMA((2,)),
            pltpu.SemaphoreType.REGULAR((8,)),
        ],
        compiler_params=pltpu.CompilerParams(
            collective_id=0, has_side_effects=True, vmem_limit_bytes=60 * 1024 * 1024
        ),
        name="exchange",
    )(by_y, x_factor, running_r)


def element(row, lane):
    return jnp.broadcast_to(row[0:1, lane:lane + 1], (ROWS, LANES))

def factor_panel(rows, lane):
    rows = list(rows)
    diag = {(k, i): element(rows[k], lane + i) for k in range(ROWS) for i in range(k, ROWS)}
    done = []
    for k in range(ROWS):
        inv = lax.rsqrt(diag[k, k])
        scaled = {i: diag[k, i] * inv for i in range(k + 1, ROWS)}
        top = rows[k] * inv
        done.append(top)
        for i in range(k + 1, ROWS):
            for j in range(i, ROWS):
                diag[i, j] = diag[i, j] - scaled[i] * scaled[j]
            rows[i] = rows[i] - scaled[i] * top
    return done

def chol_kernel(n, a_ref, u_ref, work, rowbuf, spread, upper):
    nb = -(-n // LANES); width = nb * LANES
    for t in range(nb):
        w = min(LANES, n - t * LANES)
        work[t, 0:n, 0:w] = a_ref[:, t * LANES:t * LANES + w]

    def block(b, panels, tiles):
        start = pl.multiple_of(b * LANES, LANES)
        for p in range(panels):
            for s in range(tiles):
                t = jnp.minimum(b + s, nb - 1)
                rowbuf[pl.ds(p * 64 + s, ROWS, stride=ROWS), :] = work[t, pl.ds(start + p * ROWS, ROWS), :]
        def get(i):
            return rowbuf[i * ROWS:(i + 1) * ROWS, :]
        def put(i, v):
            rowbuf[i * ROWS:(i + 1) * ROWS, :] = v
        half = panels // 2 if panels > 8 else panels
        def rest_end(p):
            return (half if p < half else panels) * ROWS
        rows = [get(i) for i in range(ROWS)]
        for p in range(panels):
            lane = p * ROWS
            done = factor_panel(rows, lane)
            for k in range(ROWS):
                put(lane + k, done[k])
            if p + 1 == panels:
                break
            if p + 1 == half:
                for q in range(half):
                    for s in range(tiles):
                        upper[s, q * ROWS:(q + 1) * ROWS, :] = rowbuf[pl.ds(q * 64 + s, ROWS, stride=ROWS), :]
                left = upper[0, :, half * ROWS:]
                for s in range(tiles):
                    change = lax.dot_general(left, upper[s], (((0,), (0,)), ((), ())), precision=HIGH, preferred_element_type=jnp.float32)
                    for q in range(half):
                        where = pl.ds((half + q) * 64 + s, ROWS, stride=ROWS)
                        rowbuf[where, :] = rowbuf[where, :] - change[q * ROWS:(q + 1) * ROWS, :]
                rows = [get(half * ROWS + i) for i in range(ROWS)]
                continue
            rows = []
            flat = rowbuf[pl.ds(lane * ROWS, ROWS, stride=ROWS), :]
            for i in range(ROWS):
                j = lane + ROWS + i
                spread[j * ROWS:(j + 1) * ROWS, :] = jnp.broadcast_to(flat[:, j:j + 1], (ROWS, LANES))
            for i in range(ROWS):
                value = get(lane + ROWS + i)
                acc = None
                for k in range(ROWS):
                    term = spread[pl.ds((lane + ROWS + i) * ROWS + k, ROWS, stride=0), :] * done[k]
                    acc = term if acc is None else acc + term
                rows.append(value - acc)
            if (p + 2) * ROWS < rest_end(p):
                for i in range((p + 2) * ROWS, rest_end(p)):
                    spread[i * ROWS:(i + 1) * ROWS, :] = jnp.broadcast_to(flat[:, i:i + 1], (ROWS, LANES))
                    acc = None
                    for k in range(ROWS):
                        term = spread[pl.ds(i * ROWS + k, ROWS, stride=0), :] * done[k]
                        acc = term if acc is None else acc + term
                    put(i, get(i) - acc)
        for p in range(panels):
            for s in range(tiles):
                t = jnp.minimum(b + s, nb - 1)
                def move():
                    work[t, pl.ds(start + p * ROWS, ROWS), :] = rowbuf[pl.ds(p * 64 + s, ROWS, stride=ROWS), :]
                pl.when(b + s < nb)(move)

    full = n // LANES
    rest = (n - full * LANES) // ROWS
    @pl.loop(0, full)
    def _(b):
        block(b, LANES // ROWS, nb)
        for static in range(full):
            if (static + 1) * LANES < n:
                @pl.when(b == static)
                def _():
                    low = static * LANES
                    for r in range(static + 1, nb):
                        hi = min((r + 1) * LANES, n)
                        left = work[r, low:low + LANES, 0:hi - r * LANES]
                        for c in range(r, nb):
                            right = work[c, low:low + LANES, :]
                            work[c, r * LANES:hi, :] -= lax.dot_general(left, right, (((0,), (0,)), ((), ())), precision=HIGH, preferred_element_type=jnp.float32)
    if rest:
        block(full, rest, 1)
    for t in range(nb):
        w = min(LANES, n - t * LANES)
        for r in range(nb):
            hi = min((r + 1) * LANES, n); lo = r * LANES
            if r < t:
                u_ref[lo:hi, t * LANES:t * LANES + w] = work[t, lo:hi, 0:w]
            elif r > t:
                u_ref[lo:hi, t * LANES:t * LANES + w] = jnp.zeros((hi - lo, w), jnp.float32)
            else:
                v = work[t, lo:hi, 0:w]
                keep = lax.broadcasted_iota(jnp.int32, v.shape, 0) <= lax.broadcasted_iota(jnp.int32, v.shape, 1)
                u_ref[lo:hi, t * LANES:t * LANES + w] = jnp.where(keep, v, 0.0)

def upper_factor(a):
    n = a.shape[0]; nb = -(-n // LANES)
    return pl.pallas_call(
        functools.partial(chol_kernel, n),
        out_shape=jax.ShapeDtypeStruct((n, n), jnp.float32),
        in_specs=[pl.BlockSpec(memory_space=pltpu.VMEM)], out_specs=pl.BlockSpec(memory_space=pltpu.VMEM),
        scratch_shapes=[pltpu.VMEM((nb, nb * LANES, LANES), jnp.float32), pltpu.VMEM((LANES * ROWS, LANES), jnp.float32), pltpu.VMEM((LANES * ROWS, LANES), jnp.float32), pltpu.VMEM((nb, LANES // 2, LANES), jnp.float32)],
        compiler_params=pltpu.CompilerParams(vmem_limit_bytes=40 * 1024 * 1024), name="factor",
    )(a)


def on_device(n_gx, n_gy, fields, x_factor, running_r):
    x_block, y_block, cells = fields.shape
    full_y = running_r.shape[0]
    plan = Plan(n_gx, n_gy, x_block, y_block, cells, x_factor.shape[1], full_y)
    total = updated_total(plan, fields, x_factor, running_r)
    upper_r = upper_factor(total)
    row_block = full_y // n_gy
    col_block = full_y // n_gx
    return lax.dynamic_slice(
        upper_r,
        (lax.axis_index("gy") * row_block, lax.axis_index("gx") * col_block),
        (row_block, col_block),
    )


def solution(mesh):
    in_specs = (P("gx", "gy", None), P(), P())
    out_specs = P("gy", "gx")
    return jax.shard_map(
        functools.partial(on_device, mesh.shape["gx"], mesh.shape["gy"]),
        mesh=mesh, in_specs=in_specs, out_specs=out_specs, check_vma=False,
    )
```
